32 devices in a mesh: groups: 2 (over y), seq: 8 (over z, x), heads: 2 (over core).
Axes of the slice: x: 2, y: 2, z: 4, core: 2. Of those that a mesh axis runs over, the one named last changes fastest.
Arguments:
- queries: bfloat16 [8192, 16, 128], P(('groups', 'seq'), 'heads'), parts along dimension 0, may hold values from -128 to 128
- keys: bfloat16 [8192, 16, 128], P(('groups', 'seq'), 'heads'), parts along dimension 0, may hold values from -128 to 128
- values: bfloat16 [8192, 16, 128], P(('groups', 'seq'), 'heads'), parts along dimension 0, may hold values from -6 to 6
Outputs:
- attended: bfloat16 [8192, 16, 128], P(('groups', 'seq'), 'heads'), parts along dimension 0
The draws below stay inside these ranges and needn't reach their ends.
There are 2 independent parts, one for each index of `groups`. The reference program is written for one: setup_inputs(seed, part) draws one part's arguments, and reference() takes and returns one part's arrays. A program takes and returns all parts, laid end to end along the dimension named above; each array names one. Nothing has to cross between parts.
All inputs are finite; a program needn't handle non-finite values.
Results may differ from the reference program's by a relative error of at most 0.0055.
Values may be sent and summed in bfloat16 or wider, within the bound.
No kernel may reach another device: no remote copies, remote signals or barrier semaphores. Data moves between devices by JAX's collectives and lax.ppermute only.
A program may use at most 128 MiB of HBM per device.

```python
import math
import jax
import jax.numpy as jnp
from jax import lax

HEADS = 16
HD = 128
BLOCK = 64
LENGTH = 4096


def paired_fields(key):
    shape = (LENGTH, HEADS, HD)
    queries = jnp.clip(jax.random.normal(jax.random.fold_in(key, 101), shape, jnp.float32), -5.0, 5.0)
    keys = jnp.clip(jax.random.normal(jax.random.fold_in(key, 102), shape, jnp.float32), -5.0, 5.0)
    return (queries, keys)


def draw_queries(key, part):
    return paired_fields(key)[0].astype(jnp.bfloat16)


def draw_keys(key, part):
    return paired_fields(key)[1].astype(jnp.bfloat16)


def block_scale(own_key, extent, shards, smallest, largest):
    factor_of, own = 1.0, jax.random.fold_in(own_key, 6)
    for axis_at, parts in shards:
        draws = jnp.exp(jax.random.uniform(jax.random.fold_in(own, axis_at), (parts,), jnp.float32, smallest / len(shards), largest / len(shards)))
        factor_of = factor_of * jnp.repeat(draws, extent[axis_at] // parts).reshape([-1 if axis == axis_at else 1 for axis in range(len(extent))])
    return factor_of


def bell_draw(stream_key, extent, scale, bound, pieces=(), kind=jnp.bfloat16):
    result = scale * jax.random.normal(stream_key, extent, jnp.float32)
    if pieces:
        result = result * block_scale(stream_key, extent, pieces, -0.22, 0.18)
    return jnp.clip(result, -bound, bound).astype(kind)


def setup_inputs(seed: int = 0, part: int = 0) -> dict:
    key_of = jax.random.split(jax.random.key(seed), 4)
    part_splits = jax.random.split(jax.random.fold_in(key_of[3], part), 4)
    return {
        "queries": draw_queries(jax.random.fold_in(jax.random.fold_in(key_of[3], part), 71), part),
        "keys": draw_keys(jax.random.fold_in(jax.random.fold_in(key_of[3], part), 71), part),
        "values": bell_draw(part_splits[2], (LENGTH, HEADS, HD), 1.0, 6.0, ((0, 8), (1, 2))),
    }


neg_big = -1e+30
log_two = math.log(2.0)

def pool_rows(block, factor):
    count = block.shape[0] // factor
    grouped = block.astype(jnp.float32).reshape(count, factor, block.shape[1], block.shape[2])
    return lax.optimization_barrier(jnp.mean(grouped, axis=1)).astype(jnp.bfloat16)

def level_scores(query_block, key_rows, valid, bias):
    scores = jnp.einsum('qhd,khd->hqk', query_block.astype(jnp.float32), key_rows.astype(jnp.float32))
    scores = scores / math.sqrt(query_block.shape[2]) + bias
    return jnp.where(valid[None], scores, neg_big)

def reference(queries, keys, values):
    length, heads, width = queries.shape
    quad = 4 * BLOCK
    padding = jnp.zeros((BLOCK, heads, width), jnp.bfloat16)
    pooled_k = [pool_rows(keys, 2 ** level) for level in (1, 2, 3)]
    pooled_v = [pool_rows(values, 2 ** level) for level in (1, 2, 3)]
    ext0_k = jnp.concatenate([padding, keys], 0)
    ext0_v = jnp.concatenate([padding, values], 0)
    ext1_k = jnp.concatenate([padding, pooled_k[0]], 0)
    ext1_v = jnp.concatenate([padding, pooled_v[0]], 0)
    ext2_k = jnp.concatenate([padding, pooled_k[1]], 0)
    ext2_v = jnp.concatenate([padding, pooled_v[1]], 0)
    coarse_rows = jnp.arange(length // 8, dtype=jnp.int32)

    def one_block(blk):
        start = (blk * quad).astype(jnp.int32)
        posit = start + jnp.arange(quad, dtype=jnp.int32)
        bound0 = (posit // BLOCK - 1) * BLOCK
        bound1 = (posit // (2 * BLOCK) - 1) * 2 * BLOCK
        bound2 = (posit // quad - 1) * quad
        query_block = lax.dynamic_slice_in_dim(queries, start, quad, 0)
        tokens0 = start - BLOCK + jnp.arange(quad + BLOCK, dtype=jnp.int32)
        rows1 = start // 2 - BLOCK + jnp.arange(quad // 2 + BLOCK, dtype=jnp.int32)
        rows2 = start // 4 - BLOCK + jnp.arange(quad // 4 + BLOCK, dtype=jnp.int32)
        key0 = lax.dynamic_slice_in_dim(ext0_k, start, quad + BLOCK, 0)
        val0 = lax.dynamic_slice_in_dim(ext0_v, start, quad + BLOCK, 0)
        key1 = lax.dynamic_slice_in_dim(ext1_k, (start // 2).astype(jnp.int32), quad // 2 + BLOCK, 0)
        val1 = lax.dynamic_slice_in_dim(ext1_v, (start // 2).astype(jnp.int32), quad // 2 + BLOCK, 0)
        key2 = lax.dynamic_slice_in_dim(ext2_k, (start // 4).astype(jnp.int32), quad // 4 + BLOCK, 0)
        val2 = lax.dynamic_slice_in_dim(ext2_v, (start // 4).astype(jnp.int32), quad // 4 + BLOCK, 0)
        valid0 = (tokens0 >= 0)[None] & (tokens0[None] >= bound0[:, None]) & (tokens0[None] <= posit[:, None])
        valid1 = (rows1 >= 0)[None] & (2 * rows1[None] >= bound1[:, None]) & (2 * rows1[None] + 2 <= bound0[:, None])
        valid2 = (rows2 >= 0)[None] & (4 * rows2[None] >= bound2[:, None]) & (4 * rows2[None] + 4 <= bound1[:, None])
        valid3 = 8 * coarse_rows[None] + 8 <= bound2[:, None]
        scores = jnp.concatenate([level_scores(query_block, key0, valid0, 0.0), level_scores(query_block, key1, valid1, log_two), level_scores(query_block, key2, valid2, 2.0 * log_two), level_scores(query_block, pooled_k[2], valid3, 3.0 * log_two)], axis=2)
        value_rows = jnp.concatenate([val0, val1, val2, pooled_v[2]], 0)
        top = lax.optimization_barrier(jnp.max(scores, axis=2, keepdims=True))
        weights = jnp.exp(scores - top)
        total = lax.optimization_barrier(jnp.sum(weights, axis=2))
        rounded = weights.astype(jnp.bfloat16)
        summed = jnp.einsum('hqk,khd->hqd', rounded.astype(jnp.float32), value_rows.astype(jnp.float32))
        return (summed / total[..., None]).transpose(1, 0, 2).astype(jnp.bfloat16)
    blocks = lax.map(one_block, jnp.arange(length // quad, dtype=jnp.int32))
    return blocks.reshape(length, heads, width)
```

```python
import functools
import math

import jax
import jax.numpy as jnp
from jax import lax
from jax.experimental import pallas as pl
from jax.experimental.pallas import tpu as pltpu
from jax.sharding import PartitionSpec as P

BLOCK = 64
QUAD = 4 * BLOCK
PAIR = 2 * BLOCK
NEG = -1e30
F32 = jnp.float32
BF16 = jnp.bfloat16
VMEM = pl.BlockSpec(memory_space=pltpu.VMEM)
SMEM = pl.BlockSpec(memory_space=pltpu.SMEM)


def shifted(value, axis, steps):
    count = lax.axis_size(axis)
    return lax.ppermute(value, axis, [(i, i + steps) for i in range(count - steps)])


def pooled(block, factor):
    count = block.shape[0] // factor
    grouped = block.reshape(count, factor, block.shape[1], block.shape[2])
    total = grouped[:, 0]
    for i in range(1, factor):
        total = total + grouped[:, i]
    return total * (1.0 / factor)


def flat(block):
    return block.reshape(block.shape[0] * block.shape[1], block.shape[2])


def prep_kernel(k_ref, v_ref, halo_ref, far_ref, tok):
    rows, heads, width = k_ref.shape
    for side, ref in enumerate((k_ref, v_ref)):
        base = 0
        for chunk in range(rows // BLOCK):
            block = ref[pl.ds(chunk * BLOCK, BLOCK)].astype(F32)
            part = flat(pooled(block, 8))
            tok[pl.ds(base, part.shape[0])] = part
            base += part.shape[0]
        near = ref[pl.ds(rows - BLOCK, BLOCK)].astype(F32)
        tok[pl.ds(base, BLOCK * heads)] = flat(near)
        level1 = pooled(ref[pl.ds(rows - 2 * BLOCK, BLOCK)].astype(F32), 2)
        tok[pl.ds(base + BLOCK * heads, BLOCK * heads // 2)] = flat(level1)
        level2 = pooled(ref[pl.ds(rows - QUAD, 2 * BLOCK)].astype(F32), 4)
        tok[pl.ds(base + BLOCK * heads * 3 // 2, BLOCK * heads // 2)] = flat(level2)
        for head in range(heads):
            far_ref[side, head] = tok[pl.ds(head, rows // 8, stride=heads)].astype(BF16)
            halo_ref[side, head] = tok[pl.ds(base + head, 2 * BLOCK, stride=heads)].astype(BF16)


def prep(keys, values):
    rows, heads, width = keys.shape
    return pl.pallas_call(
        prep_kernel,
        out_shape=(
            jax.ShapeDtypeStruct((2, heads, 2 * BLOCK, width), BF16),
            jax.ShapeDtypeStruct((2, heads, rows // 8, width), BF16),
        ),
        in_specs=[VMEM, VMEM],
        out_specs=(VMEM, VMEM),
        scratch_shapes=[pltpu.VMEM(((rows // 8 + 2 * BLOCK) * heads, width), F32)],
        name="prep",
    )(keys, values)


def local_kernel(me_ref, q_ref, k_ref, v_ref, halo_ref, qh_ref, acc_ref, stat_ref, tok, tmp, bias, *ext):
    rows, heads, width = k_ref.shape
    scale = math.log2(math.e) / math.sqrt(width)
    pairs = rows // PAIR
    first = me_ref[0] == 0
    columns = 5 * BLOCK

    def spread(ref, factor, target, lead):
        for chunk in range(rows // BLOCK):
            block = ref[pl.ds(chunk * BLOCK, BLOCK)].astype(F32)
            part = flat(block if factor == 1 else pooled(block, factor))
            tok[pl.ds(chunk * part.shape[0], part.shape[0])] = part
        for head in range(heads):
            target[head, pl.ds(lead, rows // factor)] = tok[pl.ds(head, rows // factor, stride=heads)].astype(BF16)

    spread(q_ref, 1, qh_ref, 0)
    for side, ref in enumerate((k_ref, v_ref)):
        ext0, ext1, ext2 = ext[3 * side : 3 * side + 3]
        spread(ref, 1, ext0, BLOCK)
        spread(ref, 2, ext1, BLOCK)
        spread(ref, 4, ext2, BLOCK)
        for head in range(heads):
            near = halo_ref[side, head, :BLOCK]
            level1 = halo_ref[side, head, BLOCK : BLOCK * 3 // 2]
            tmp[:BLOCK] = near.astype(F32)
            tmp[BLOCK : BLOCK * 3 // 2] = level1.astype(F32)
            ext0[head, :BLOCK] = near
            ext1[head, : BLOCK // 2] = level1
            ext1[head, BLOCK // 2 : BLOCK] = (
                (tmp[pl.ds(0, BLOCK // 2, stride=2)] + tmp[pl.ds(1, BLOCK // 2, stride=2)]) * 0.5
            ).astype(BF16)
            ext2[head, : BLOCK // 2] = halo_ref[side, head, BLOCK * 3 // 2 :]
            ext2[head, BLOCK // 2 : BLOCK * 3 // 4] = (
                (tmp[pl.ds(BLOCK, BLOCK // 4, stride=2)] + tmp[pl.ds(BLOCK + 1, BLOCK // 4, stride=2)]) * 0.5
            ).astype(BF16)
            ext2[head, BLOCK * 3 // 4 : BLOCK] = (
                (
                    (tmp[pl.ds(0, BLOCK // 4, stride=4)] + tmp[pl.ds(1, BLOCK // 4, stride=4)])
                    + (tmp[pl.ds(2, BLOCK // 4, stride=4)] + tmp[pl.ds(3, BLOCK // 4, stride=4)])
                )
                * 0.25
            ).astype(BF16)

    row = lax.broadcasted_iota(jnp.int32, (PAIR, columns), 0)
    col = lax.broadcasted_iota(jnp.int32, (PAIR, columns), 1)
    late = row >= BLOCK
    is0 = col < 3 * BLOCK
    is1 = (col >= 3 * BLOCK) & (col < 4 * BLOCK)
    is2 = col >= 4 * BLOCK
    ok0 = is0 & (col - BLOCK <= row) & ((col >= BLOCK) | ~late)
    ok1 = is1 & ((col < 3 * BLOCK + BLOCK // 2) | late)
    for pair in range(4):
        ok2 = is2 & (col < 4 * BLOCK + BLOCK // 2) if pair % 2 == 0 else is2
        ok = ok0 | ok1 | ok2
        if pair == 0:
            ok = ok & ((is0 & (col >= BLOCK)) | ~first)
        if pair == 1:
            ok = ok & (~is2 | ~first)
        level = jnp.where(is0, 0.0, jnp.where(is1, 1.0, 2.0))
        bias[pair] = jnp.where(ok, level, NEG)

    lane = lax.broadcasted_iota(jnp.int32, (PAIR, width), 1)
    for pair in range(pairs):
        kind = pair if pair < 2 else 2 + pair % 2
        base2 = pair // 2 * BLOCK

        def one_head(head, stats):
            def rows_of(side):
                ext0, ext1, ext2 = ext[3 * side : 3 * side + 3]
                return jnp.concatenate(
                    [
                        ext0[head, pl.ds(PAIR * pair, 3 * BLOCK)],
                        ext1[head, pl.ds(BLOCK * pair, BLOCK)],
                        ext2[head, pl.ds(base2, BLOCK)],
                    ],
                    0,
                )

            query = qh_ref[head, pl.ds(PAIR * pair, PAIR)]
            score = lax.dot_general(query, rows_of(0), (((1,), (1,)), ((), ())), preferred_element_type=F32)
            score = score * scale + bias[kind]
            top = jnp.max(score, axis=1, keepdims=True)
            weight = jnp.exp2(score - top)
            total = jnp.sum(weight, axis=1, keepdims=True)
            acc_ref[head, pl.ds(PAIR * pair, PAIR)] = jnp.dot(
                weight.astype(BF16), rows_of(1), preferred_element_type=F32
            )
            stats = jnp.where(lane == head, top, stats)
            return jnp.where(lane == head + heads, total, stats)

        stats = jnp.zeros((PAIR, width), F32)
        for head in range(heads):
            stats = one_head(head, stats)
        stat_ref[pl.ds(PAIR * pair, PAIR)] = stats


def local(me, queries, keys, values, halo):
    rows, heads, width = keys.shape
    side = [
        pltpu.VMEM((heads, BLOCK + rows // factor, width), BF16) for factor in (1, 2, 4)
    ]
    return pl.pallas_call(
        local_kernel,
        out_shape=(
            jax.ShapeDtypeStruct((heads, rows, width), BF16),
            jax.ShapeDtypeStruct((heads, rows, width), F32),
            jax.ShapeDtypeStruct((rows, width), F32),
        ),
        in_specs=[SMEM, VMEM, VMEM, VMEM, VMEM],
        out_specs=(VMEM, VMEM, VMEM),
        scratch_shapes=[
            pltpu.VMEM((rows * heads, width), F32),
            pltpu.VMEM((BLOCK * 3 // 2, width), F32),
            pltpu.VMEM((4, PAIR, 5 * BLOCK), F32),
        ]
        + side
        + side,
        name="local",
    )(me, queries, keys, values, halo)


def far_kernel(sources, me_ref, qh_ref, acc_ref, stat_ref, *refs):
    chunks, (out_ref, tok) = refs[:-2], refs[-2:]
    heads, tile, width = qh_ref.shape
    count = chunks[0].shape[-2]
    scale = math.log2(math.e) / math.sqrt(width)
    me = me_ref[0]
    quad = pl.program_id(0) * tile // QUAD
    limit = me * count + (quad - 1) * (QUAD // 8)
    columns = count * len(chunks)
    col = lax.broadcasted_iota(jnp.int32, (1, columns), 1)
    bias = jnp.full((1, columns), NEG, F32)
    for at, back in enumerate(sources):
        ours = (col >= at * count) & (col < (at + 1) * count)
        number = (me - back) * count + col - at * count
        ours = ours & (number < limit) & (me >= back)
        bias = jnp.where(ours, 3.0, bias)
    for head in range(heads):
        kept = jnp.concatenate([chunk[0, head] for chunk in chunks], 0)
        score = lax.dot_general(qh_ref[head], kept, (((1,), (1,)), ((), ())), preferred_element_type=F32)
        score = score * scale + bias
        before = stat_ref[:, head : head + 1]
        top = jnp.maximum(before, jnp.max(score, axis=1, keepdims=True))
        fade = jnp.exp2(before - top)
        weight = jnp.exp2(score - top)
        total = stat_ref[:, heads + head : heads + head + 1] * fade + jnp.sum(weight, axis=1, keepdims=True)
        kept = jnp.concatenate([chunk[1, head] for chunk in chunks], 0)
        summed = acc_ref[head] * fade + jnp.dot(weight.astype(BF16), kept, preferred_element_type=F32)
        tok[pl.ds(head, tile, stride=heads)] = summed * (1.0 / total)
    out_ref[...] = tok[...].reshape(tile, heads, width).astype(BF16)


def far(me, qh, acc, stat, chunks, sources):
    heads, rows, width = qh.shape
    tile = PAIR
    return pl.pallas_call(
        functools.partial(far_kernel, sources),
        out_shape=jax.ShapeDtypeStruct((rows, heads, width), BF16),
        grid=(rows // tile,),
        in_specs=[
            SMEM,
            pl.BlockSpec((heads, tile, width), lambda i: (0, i, 0)),
            pl.BlockSpec((heads, tile, width), lambda i: (0, i, 0)),
            pl.BlockSpec((tile, width), lambda i: (i, 0)),
        ]
        + [VMEM] * len(chunks),
        out_specs=pl.BlockSpec((tile, heads, width), lambda i: (i, 0, 0)),
        scratch_shapes=[pltpu.VMEM((tile * heads, width), F32)],
        name="far",
    )(me, qh, acc, stat, *chunks)


def shards(queries, keys, values):
    count = lax.axis_size("seq")
    me = lax.axis_index("seq").reshape(1)
    halo, own = prep(keys, values)
    halo = shifted(halo, "seq", 1)
    sources = tuple(range(1, count))
    chunks = [shifted(own, "seq", back) for back in sources]
    qh, acc, stat = local(me, queries, keys, values, halo)
    return far(me, qh, acc, stat, chunks, sources)


def solution(mesh):
    spec = P(("groups", "seq"), "heads", None)
    return jax.shard_map(
        shards,
        mesh=mesh,
        in_specs=(spec, spec, spec),
        out_specs=spec,
        check_vma=False,
    )
```

```python
import functools
import math

import jax
import jax.numpy as jnp
from jax import lax
from jax.experimental import pallas as pl
from jax.experimental.pallas import tpu as pltpu
from jax.sharding import PartitionSpec as P

BLOCK = 64
QUAD = 4 * BLOCK
PAIR = 2 * BLOCK
NEG = -1e30
F32 = jnp.float32
BF16 = jnp.bfloat16
VMEM = pl.BlockSpec(memory_space=pltpu.VMEM)
SMEM = pl.BlockSpec(memory_space=pltpu.SMEM)


def shifted(value, axis, steps):
    count = lax.axis_size(axis)
    return lax.ppermute(value, axis, [(i, i + steps) for i in range(count - steps)])


def pooled(block, factor):
    count = block.shape[0] // factor
    grouped = block.reshape(count, factor, block.shape[1], block.shape[2])
    total = grouped[:, 0]
    for i in range(1, factor):
        total = total + grouped[:, i]
    return total * (1.0 / factor)


def flat(block):
    return block.reshape(block.shape[0] * block.shape[1], block.shape[2])


def prep_kernel(k_ref, v_ref, halo_ref, far_ref, tok):
    rows, heads, width = k_ref.shape
    for side, ref in enumerate((k_ref, v_ref)):
        base = 0
        for chunk in range(rows // BLOCK):
            block = ref[pl.ds(chunk * BLOCK, BLOCK)].astype(F32)
            part = flat(pooled(block, 8))
            tok[pl.ds(base, part.shape[0])] = part
            base += part.shape[0]
        near = ref[pl.ds(rows - BLOCK, BLOCK)].astype(F32)
        tok[pl.ds(base, BLOCK * heads)] = flat(near)
        level1 = pooled(ref[pl.ds(rows - 2 * BLOCK, BLOCK)].astype(F32), 2)
        tok[pl.ds(base + BLOCK * heads, BLOCK * heads // 2)] = flat(level1)
        level2 = pooled(ref[pl.ds(rows - QUAD, 2 * BLOCK)].astype(F32), 4)
        tok[pl.ds(base + BLOCK * heads * 3 // 2, BLOCK * heads // 2)] = flat(level2)
        for head in range(heads):
            far_ref[side, head] = tok[pl.ds(head, rows // 8, stride=heads)].astype(BF16)
            halo_ref[side, head] = tok[pl.ds(base + head, 2 * BLOCK, stride=heads)].astype(BF16)


def prep(keys, values):
    rows, heads, width = keys.shape
    return pl.pallas_call(
        prep_kernel,
        out_shape=(
            jax.ShapeDtypeStruct((2, heads, 2 * BLOCK, width), BF16),
            jax.ShapeDtypeStruct((2, heads, rows // 8, width), BF16),
        ),
        in_specs=[VMEM, VMEM],
        out_specs=(VMEM, VMEM),
        scratch_shapes=[pltpu.VMEM(((rows // 8 + 2 * BLOCK) * heads, width), F32)],
        compiler_params=pltpu.CompilerParams(vmem_limit_bytes=28 << 20),
        name="prep",
    )(keys, values)


def local_kernel(me_ref, q_ref, k_ref, v_ref, halo_ref, qh_ref, acc_ref, top_ref, tok, tmp, bias, *ext):
    rows, heads, width = k_ref.shape
    scale = math.log2(math.e) / math.sqrt(width)
    pairs = rows // PAIR
    first = me_ref[0] == 0
    columns = 5 * BLOCK

    for chunk in range(rows // BLOCK):
        tok[pl.ds(chunk * BLOCK * heads, BLOCK * heads)] = flat(q_ref[pl.ds(chunk * BLOCK, BLOCK)].astype(F32))
    for head in range(heads):
        qh_ref[head] = tok[pl.ds(head, rows, stride=heads)].astype(BF16)
    for side, ref in enumerate((k_ref, v_ref)):
        ext0, ext1, ext2 = ext[3 * side : 3 * side + 3]
        for chunk in range(rows // BLOCK):
            block = ref[pl.ds(chunk * BLOCK, BLOCK)].astype(F32)
            tok[pl.ds(chunk * BLOCK * heads, BLOCK * heads)] = flat(block)
            for factor, base in ((2, rows), (4, rows * 3 // 2)):
                part = flat(pooled(block, factor))
                tok[pl.ds(base * heads + chunk * part.shape[0], part.shape[0])] = part
        for head in range(heads):
            for factor, base, target in ((1, 0, ext0), (2, rows, ext1), (4, rows * 3 // 2, ext2)):
                target[head, pl.ds(BLOCK, rows // factor)] = tok[
                    pl.ds(base * heads + head, rows // factor, stride=heads)
                ].astype(BF16)
            near = halo_ref[side, head, :BLOCK]
            level1 = halo_ref[side, head, BLOCK : BLOCK * 3 // 2]
            tmp[:BLOCK] = near.astype(F32)
            tmp[BLOCK : BLOCK * 3 // 2] = level1.astype(F32)
            ext0[head, :BLOCK] = near
            ext1[head, : BLOCK // 2] = level1
            ext1[head, BLOCK // 2 : BLOCK] = (
                (tmp[pl.ds(0, BLOCK // 2, stride=2)] + tmp[pl.ds(1, BLOCK // 2, stride=2)]) * 0.5
            ).astype(BF16)
            ext2[head, : BLOCK // 2] = halo_ref[side, head, BLOCK * 3 // 2 :]
            ext2[head, BLOCK // 2 : BLOCK * 3 // 4] = (
                (tmp[pl.ds(BLOCK, BLOCK // 4, stride=2)] + tmp[pl.ds(BLOCK + 1, BLOCK // 4, stride=2)]) * 0.5
            ).astype(BF16)
            ext2[head, BLOCK * 3 // 4 : BLOCK] = (
                (
                    (tmp[pl.ds(0, BLOCK // 4, stride=4)] + tmp[pl.ds(1, BLOCK // 4, stride=4)])
                    + (tmp[pl.ds(2, BLOCK // 4, stride=4)] + tmp[pl.ds(3, BLOCK // 4, stride=4)])
                )
                * 0.25
            ).astype(BF16)

    row = lax.broadcasted_iota(jnp.int32, (PAIR, columns), 0)
    col = lax.broadcasted_iota(jnp.int32, (PAIR, columns), 1)
    late = row >= BLOCK
    is0 = col < 3 * BLOCK
    is1 = (col >= 3 * BLOCK) & (col < 4 * BLOCK)
    is2 = col >= 4 * BLOCK
    ok0 = is0 & (col - BLOCK <= row) & ((col >= BLOCK) | ~late)
    ok1 = is1 & ((col < 3 * BLOCK + BLOCK // 2) | late)
    for pair in range(4):
        ok2 = is2 & (col < 4 * BLOCK + BLOCK // 2) if pair % 2 == 0 else is2
        ok = ok0 | ok1 | ok2
        if pair == 0:
            ok = ok & ((is0 & (col >= BLOCK)) | ~first)
        if pair == 1:
            ok = ok & (~is2 | ~first)
        level = jnp.where(is0, 0.0, jnp.where(is1, 1.0, 2.0))
        bias[pair] = jnp.where(ok, level, NEG)

    ones = jnp.ones((columns, width), BF16)
    for pair in range(pairs):
        kind = pair if pair < 2 else 2 + pair % 2
        base2 = pair // 2 * BLOCK

        def rows_of(side, head):
            ext0, ext1, ext2 = ext[3 * side : 3 * side + 3]
            return jnp.concatenate(
                [
                    ext0[head, pl.ds(PAIR * pair, 3 * BLOCK)],
                    ext1[head, pl.ds(BLOCK * pair, BLOCK)],
                    ext2[head, pl.ds(base2, BLOCK)],
                ],
                0,
            )

        for head in range(heads):
            query = qh_ref[head, pl.ds(PAIR * pair, PAIR)]
            score = lax.dot_general(query, rows_of(0, head), (((1,), (1,)), ((), ())), preferred_element_type=F32)
            score = score * scale + bias[kind]
            top = jnp.max(score, axis=1, keepdims=True)
            weight = jnp.exp2(score - top).astype(BF16)
            kept = jnp.concatenate([rows_of(1, head), ones], 1)
            acc_ref[head, pl.ds(PAIR * pair, PAIR)] = jnp.dot(weight, kept, preferred_element_type=F32)
            top_ref[head, pl.ds(PAIR * pair, PAIR)] = jnp.broadcast_to(top, (PAIR, width))


def local(me, queries, keys, values, halo):
    rows, heads, width = keys.shape
    side = [
        pltpu.VMEM((heads, BLOCK + rows // factor, width), BF16) for factor in (1, 2, 4)
    ]
    return pl.pallas_call(
        local_kernel,
        out_shape=(
            jax.ShapeDtypeStruct((heads, rows, width), BF16),
            jax.ShapeDtypeStruct((heads, rows, 2 * width), F32),
            jax.ShapeDtypeStruct((heads, rows, width), F32),
        ),
        in_specs=[SMEM, VMEM, VMEM, VMEM, VMEM],
        out_specs=(VMEM, VMEM, VMEM),
        scratch_shapes=[
            pltpu.VMEM((rows * 7 // 4 * heads, width), F32),
            pltpu.VMEM((BLOCK * 3 // 2, width), F32),
            pltpu.VMEM((4, PAIR, 5 * BLOCK), F32),
        ]
        + side
        + side,
        compiler_params=pltpu.CompilerParams(vmem_limit_bytes=28 << 20),
        name="local",
    )(me, queries, keys, values, halo)


def far_kernel(sources, me_ref, qh_ref, acc_ref, top_ref, *refs):
    chunks, (out_ref, tok) = refs[:-2], refs[-2:]
    heads, rows, width = qh_ref.shape
    count = chunks[0].shape[-2]
    scale = math.log2(math.e) / math.sqrt(width)
    me = me_ref[0]
    some = me > 0
    step = QUAD // 8
    ones = jnp.ones((count, width), BF16)
    for quad in range(rows // QUAD):
        limit = me * count + (quad - 1) * step
        at = pl.ds(quad * QUAD, QUAD)
        for head in range(heads):
            spare = jnp.concatenate([chunks[0][0, head, :step]] * (count // step), 0)
            far_k, far_v = [], []
            for chunk, back in zip(chunks, sources):
                start = (me - back) * count
                for sub in range(count // step):
                    good = (start >= 0) & (start + sub * step < limit)
                    here = pl.ds(sub * step, step)
                    far_k.append(jnp.where(good, chunk[0, head, here], spare[:step]))
                    pair = jnp.concatenate([chunk[1, head, here], ones[:step]], 1)
                    far_v.append(jnp.where(good, pair, jnp.zeros_like(pair)))
            score = lax.dot_general(
                qh_ref[head, at], jnp.concatenate(far_k, 0), (((1,), (1,)), ((), ())), preferred_element_type=F32
            )
            best = jnp.max(score, axis=1, keepdims=True)
            best = jnp.where(some, best * scale + 3.0, NEG)
            before = top_ref[head, at]
            top = jnp.maximum(before, best)
            fade = jnp.exp2(before - top)
            weight = jnp.exp2(score * scale - (top[:, :1] - 3.0)).astype(BF16)
            summed = jnp.dot(weight, jnp.concatenate(far_v, 0), preferred_element_type=F32)
            upper = acc_ref[head, at, :width] * fade + summed[:, :width]
            lower = acc_ref[head, at, width:] * fade + summed[:, width:]
            tok[pl.ds(quad * QUAD * heads + head, QUAD, stride=heads)] = upper / lower
        out_ref[at] = tok[pl.ds(quad * QUAD * heads, QUAD * heads)].reshape(QUAD, heads, width).astype(BF16)


def far(me, qh, acc, top, chunks, sources):
    heads, rows, width = qh.shape
    return pl.pallas_call(
        functools.partial(far_kernel, sources),
        out_shape=jax.ShapeDtypeStruct((rows, heads, width), BF16),
        in_specs=[SMEM, VMEM, VMEM, VMEM] + [VMEM] * len(chunks),
        out_specs=VMEM,
        scratch_shapes=[pltpu.VMEM((rows * heads, width), F32)],
        compiler_params=pltpu.CompilerParams(vmem_limit_bytes=28 << 20),
        name="far",
    )(me, qh, acc, top, *chunks)


def shards(queries, keys, values):
    count = lax.axis_size("seq")
    me = lax.axis_index("seq").reshape(1)
    halo, own = prep(keys, values)
    halo = shifted(halo, "seq", 1)
    sources = tuple(range(1, count))
    chunks = [shifted(own, "seq", back) for back in sources]
    qh, acc, stat = local(me, queries, keys, values, halo)
    return far(me, qh, acc, stat, chunks, sources)


def solution(mesh):
    spec = P(("groups", "seq"), "heads", None)
    return jax.shard_map(
        shards,
        mesh=mesh,
        in_specs=(spec, spec, spec),
        out_specs=spec,
        check_vma=False,
    )
```
